512 devices in a mesh: xy: 32 (over z, x_lo, core), gz: 16 (over y, x_hi).
Axes of the slice: x: 4 (x_hi: 2, x_lo: 2; x = x_hi * 2 + x_lo), y: 8, z: 8, core: 2. Of those that a mesh axis runs over, the one named last changes fastest.
Arguments:
- volume: bfloat16 [64, 128, 128, 128], P('xy', None, 'gz'), may hold values from -6 to 6
- conv_first: bfloat16 [3, 3, 128, 128], replicated, may hold values from -0.1875 to 0.1875
- conv_second: bfloat16 [3, 3, 128, 128], replicated, may hold values from -0.1875 to 0.1875
- w_qkv: bfloat16 [128, 384], replicated
- w_out: bfloat16 [128, 128], replicated, may hold values from -0.5 to 0.5
Outputs:
- refined: bfloat16 [64, 128, 128, 128], P('xy', None, 'gz')
The draws below stay inside these ranges and needn't reach their ends.
All inputs are finite; a program needn't handle non-finite values.
Results may differ from the reference program's by a relative error of at most 0.0085.
Values may be sent and summed in bfloat16 or wider, within the bound.
No kernel may reach another device: no remote copies, remote signals or barrier semaphores. Data moves between devices by JAX's collectives and lax.ppermute only.
A program may use at most 64 MiB of HBM per device.

```python
import math
import jax
import jax.numpy as jnp
from jax import lax

CH = 128
HEADS = 4
WIDE = 128
ROWS = 64
SECTIONS = 128


def draw_w_qkv(key, part):
    base = jax.random.normal(key, (CH, 3 * CH), jnp.float32) / math.sqrt(CH)
    return base.astype(jnp.bfloat16)


def block_scale(key, dims, split, low, top_value):
    loudness = 1.0
    for axis_at, blocks in split:
        heights = jax.random.uniform(jax.random.fold_in(jax.random.fold_in(key, 6), axis_at), (blocks,), jnp.float32, low / len(split), top_value / len(split))
        loudness = loudness * jnp.repeat(jnp.exp(heights), dims[axis_at] // blocks).reshape((-1,) + (1,) * (len(dims) - 1 - axis_at))
    return loudness


def bell_draw(stream_key, dims, deviation, limit, pieces=(), kind=jnp.bfloat16):
    loudness = block_scale(stream_key, dims, pieces, -0.22, 0.18) if pieces else 1.0
    entries = jax.random.normal(stream_key, dims, jnp.float32) * deviation * loudness
    return jnp.minimum(jnp.maximum(entries, -limit), limit).astype(kind)


def setup_inputs(seed: int = 0) -> dict:
    streams_of = jax.random.split(jax.random.key(seed), 6)
    return {
        "volume": bell_draw(streams_of[0], (ROWS, WIDE, SECTIONS, CH), 1.0, 6.0, ((0, 32), (2, 16))),
        "conv_first": bell_draw(streams_of[1], (3, 3, CH, CH), (9 * CH) ** -0.5, 0.1875),
        "conv_second": bell_draw(streams_of[2], (3, 3, CH, CH), (9 * CH) ** -0.5, 0.1875),
        "w_qkv": draw_w_qkv(jax.random.fold_in(streams_of[5], 71), 0),
        "w_out": bell_draw(streams_of[4], (CH, CH), CH ** -0.5, 0.5),
    }


def conv_all(field, weight, finish):
    count = field.shape[0]
    cols = field.shape[1]
    padded = jnp.pad(field, ((1, 1), (1, 1), (0, 0), (0, 0)))

    def one_row(index):
        rows = lax.dynamic_slice_in_dim(padded, index, 3, 0)
        total = jnp.zeros(field.shape[1:], jnp.float32)
        for shift_r in range(3):
            for shift_c in range(3):
                total = total + jnp.dot(rows[shift_r, shift_c:shift_c + cols], weight[shift_r, shift_c], preferred_element_type=jnp.float32)
        return finish(total, index)
    return lax.map(one_row, jnp.arange(count, dtype=jnp.int32))

def attend_row(row, w_qkv, w_out):
    cols, depth, width = row.shape
    values = row.astype(jnp.float32)
    normed = values / jnp.sqrt(lax.optimization_barrier(jnp.mean(values * values, axis=-1, keepdims=True)) + 1e-06)
    qkv = jnp.dot(normed.reshape(cols * depth, width), w_qkv.astype(jnp.float32), preferred_element_type=jnp.float32).astype(jnp.bfloat16)
    qkv = qkv.reshape(cols, depth, 3, HEADS, width // HEADS).astype(jnp.float32)
    scores = jnp.einsum('cqhd,ckhd->chqk', qkv[:, :, 0], qkv[:, :, 1]) / jnp.sqrt(jnp.float32(width // HEADS))
    probs = jax.nn.softmax(scores, axis=-1).astype(jnp.bfloat16)
    context = jnp.einsum('chqk,ckhd->cqhd', probs.astype(jnp.float32), qkv[:, :, 2]).astype(jnp.bfloat16)
    attended = jnp.dot(context.reshape(cols * depth, width), w_out, preferred_element_type=jnp.float32).astype(jnp.bfloat16)
    return attended.reshape(cols, depth, width)

def reference(volume, conv_first, conv_second, w_qkv, w_out):
    hidden = conv_all(volume, conv_first, lambda total, index: jax.nn.silu(total).astype(jnp.bfloat16))

    def add_back(total, index):
        base = lax.dynamic_index_in_dim(volume, index, 0, keepdims=False)
        return (base.astype(jnp.float32) + total).astype(jnp.bfloat16)
    mixed = conv_all(hidden, conv_second, add_back)

    def finish_row(row):
        attended = attend_row(row, w_qkv, w_out)
        return (row.astype(jnp.float32) + attended.astype(jnp.float32)).astype(jnp.bfloat16)
    return lax.map(finish_row, mixed)
```

```python
import functools

import jax
import jax.numpy as jnp
from jax import lax
from jax.experimental import pallas as pl
from jax.experimental.pallas import tpu as pltpu
from jax.sharding import PartitionSpec as P

HEADS=4
F32=jnp.float32; BF=jnp.bfloat16

def blocks(weight):
    zero = jnp.zeros_like(weight[0])
    top = jnp.concatenate([jnp.concatenate([weight[0], zero], -1), jnp.concatenate([weight[1], weight[0]], -1)], -2)
    low = jnp.concatenate([jnp.concatenate([weight[2], weight[1]], -1), jnp.concatenate([zero, weight[2]], -1)], -2)
    ch2 = top.shape[-1]
    return jnp.concatenate([top.reshape(-1, ch2), low.reshape(-1, ch2)], 0)

def conv_kernel(tile, groups, edge, lo_ref, mid_ref, hi_ref, wa_ref, wb_ref, out_ref, xa, xs, ha, hs, wf1, wf2):
    cols, depth, ch = mid_ref.shape[1:]
    m = cols * depth
    for w_ref, wf in ((wa_ref, wf1), (wb_ref, wf2)):
        z = jnp.zeros((ch, ch), BF)
        for dc in range(3):
            b = dc * 2 * ch
            wf[b:b+ch, :ch] = w_ref[0, dc]
            wf[b:b+ch, ch:] = z
            wf[b+ch:b+2*ch, :ch] = w_ref[1, dc]
            wf[b+ch:b+2*ch, ch:] = w_ref[0, dc]
            b += 6 * ch
            wf[b:b+ch, :ch] = w_ref[2, dc]
            wf[b:b+ch, ch:] = w_ref[1, dc]
            wf[b+ch:b+2*ch, :ch] = z
            wf[b+ch:b+2*ch, ch:] = w_ref[2, dc]
    zrow = jnp.zeros((1, depth, ch), F32)
    srcs = [lo_ref.at[0], lo_ref.at[1], mid_ref.at[0], mid_ref.at[1], hi_ref.at[0], hi_ref.at[1]]
    for r, src in enumerate(srcs):
        v = src[...].astype(F32)
        xa[r] = v.reshape(m, ch).astype(BF)
        xs[r] = jnp.concatenate([zrow, v, zrow], 0).reshape(m + 2*depth, ch).astype(BF)
    steps = m // tile
    def gather(a, s, p, t):
        parts = []
        for dc in range(3):
            for r in (2*p, 2*p+1):
                if dc == 0: parts.append(s[r, pl.ds(t, tile)])
                elif dc == 1: parts.append(a[r, pl.ds(t, tile)])
                else: parts.append(s[r, pl.ds(t + 2*depth, tile)])
        return parts
    def conv(a, s, wf, p, t):
        lhs = jnp.concatenate(gather(a, s, p, t) + gather(a, s, p+1, t), axis=-1)
        return jnp.dot(lhs, wf[...], preferred_element_type=F32)
    for p in range(2):
        keep = edge[p]
        for k in range(steps):
            t = k * tile
            acc = conv(xa, xs, wf1, p, t)
            h = acc * (1.0 / (1.0 + jnp.exp(-acc)))
            for half in range(2):
                r = 2*p + half
                v = h[:, half*ch:(half+1)*ch]
                if r in (0, 3):
                    v = v * keep
                vb = v.astype(BF)
                ha[r, pl.ds(t, tile)] = vb
                hs[r, pl.ds(t + depth, tile)] = vb
    for r in range(4):
        hs[r, pl.ds(0, depth)] = jnp.zeros((depth, ch), BF)
        hs[r, pl.ds(m + depth, depth)] = jnp.zeros((depth, ch), BF)
    for k in range(steps):
        t = k * tile
        acc = conv(ha, hs, wf2, 0, t)
        c0 = t // depth
        nc = tile // depth
        for r in range(2):
            base = mid_ref[r, pl.ds(c0, nc)].astype(F32)
            res = base + acc[:, r*ch:(r+1)*ch].reshape(nc, depth, ch)
            res = res.astype(BF)
            g = cols // groups
            for j in range(nc // g):
                out_ref[c0 // g + j, r] = res[j*g:(j+1)*g]

def conv_block(lo, mid, hi, edge, conv_first, conv_second, groups=16, tile=256):
    rows, cols, depth, ch = mid.shape
    m = cols*depth
    vm = pl.BlockSpec(memory_space=pltpu.VMEM)
    return pl.pallas_call(
        functools.partial(lambda e, *r: conv_kernel(tile, groups, e, *r)),
        out_shape=jax.ShapeDtypeStruct((groups, rows, cols//groups, depth, ch), BF),
        in_specs=[pl.BlockSpec(memory_space=pltpu.SMEM)] + [vm]*5,
        out_specs=vm,
        scratch_shapes=[pltpu.VMEM((6, m, ch), BF), pltpu.VMEM((6, m+2*depth, ch), BF),
                        pltpu.VMEM((4, m, ch), BF), pltpu.VMEM((4, m+2*depth, ch), BF),
                        pltpu.VMEM((12*ch, 2*ch), BF), pltpu.VMEM((12*ch, 2*ch), BF)],
        compiler_params=pltpu.CompilerParams(vmem_limit_bytes=48<<20),
        name="conv_block",
    )(edge, lo, mid, hi, conv_first, conv_second)

def attend_kernel(x_ref, wq_ref, wo_ref, out_ref):
    parts, rows, cols, depth, ch = x_ref.shape
    sect = parts*depth
    hd = ch // HEADS
    scale = 1.4426950408889634 / (hd ** 0.5)
    lane = lax.broadcasted_iota(jnp.int32, (1, ch), 1) // hd
    masks = [(lane == h).astype(BF) for h in range(HEADS)]
    ones = jnp.concatenate([jnp.broadcast_to(mk, (sect, ch)) for mk in masks], 0)
    def cell(r, c):
        x = x_ref[:, r, c].astype(F32).reshape(sect, ch)
        n = (x * lax.rsqrt(jnp.mean(x*x, -1, keepdims=True) + 1e-6)).astype(BF)
        qkv = jnp.dot(n, wq_ref[...], preferred_element_type=F32).astype(BF)
        q, k, v = qkv[:, :ch], qkv[:, ch:2*ch], qkv[:, 2*ch:]
        ks = jnp.concatenate([k*mk for mk in masks], 0)
        vs = jnp.concatenate([v*mk for mk in masks], 0)
        s = lax.dot_general(q, ks, (((1,), (1,)), ((), ())), preferred_element_type=F32)
        ps = []
        for h in range(HEADS):
            sh = s[:, h*sect:(h+1)*sect]
            ps.append(jnp.exp2((sh - jnp.max(sh, -1, keepdims=True)) * scale).astype(BF))
        p = jnp.concatenate(ps, 1)
        pv = jnp.dot(p, jnp.concatenate([vs, ones], 1), preferred_element_type=F32)
        ctx = (pv[:, :ch] / pv[:, ch:]).astype(BF)
        o = jnp.dot(ctx, wo_ref[...], preferred_element_type=F32)
        out_ref[:, r, c] = o.reshape(parts, depth, ch).astype(BF)
    for r in range(rows):
        for c in range(cols):
            cell(r, c)

def attend_block(x, w_qkv, w_out):
    vm = pl.BlockSpec(memory_space=pltpu.VMEM)
    return pl.pallas_call(
        attend_kernel, out_shape=jax.ShapeDtypeStruct(x.shape, BF),
        in_specs=[vm]*3, out_specs=vm,
        compiler_params=pltpu.CompilerParams(vmem_limit_bytes=48<<20), name="attend_block",
    )(x, w_qkv, w_out)


def on_device(volume, conv_first, conv_second, w_qkv, w_out):
    count, groups = lax.axis_size("xy"), lax.axis_size("gz")
    forward = [(i, i + 1) for i in range(count - 1)]
    backward = [(target, source) for source, target in forward]
    low = lax.ppermute(volume, "xy", forward)
    high = lax.ppermute(volume, "xy", backward)
    place = lax.axis_index("xy")
    edge = jnp.stack([place > 0, place < count - 1]).astype(F32)
    mixed = conv_block(low, volume, high, edge, conv_first, conv_second, groups)
    arrived = lax.all_to_all(mixed, "gz", 0, 0, tiled=True)
    attended = attend_block(arrived, w_qkv, w_out)
    returned = lax.all_to_all(attended, "gz", 0, 0, tiled=True)
    total = (mixed.astype(F32) + returned.astype(F32)).astype(BF)
    return total.transpose(1, 0, 2, 3, 4).reshape(volume.shape)


def solution(mesh):
    placed = (P("xy", None, "gz", None), P(), P(), P(), P())
    return jax.shard_map(
        on_device, mesh=mesh, in_specs=placed, out_specs=P("xy", None, "gz", None), check_vma=False
    )
```

```python
import functools

import jax
import jax.numpy as jnp
from jax import lax
from jax.experimental import pallas as pl
from jax.experimental.pallas import tpu as pltpu
from jax.sharding import PartitionSpec as P

HEADS = 4
GROUP = 8
F32 = jnp.float32
BF = jnp.bfloat16


def vmem():
    return pl.BlockSpec(memory_space=pltpu.VMEM)


def cost(flops, moved):
    return pl.CostEstimate(flops=flops, bytes_accessed=moved, transcendentals=0)


def params():
    return pltpu.CompilerParams(vmem_limit_bytes=24 << 20)


def spread(value, flat, wide):
    cols, depth, ch = value.shape
    edge = jnp.zeros((1, depth, ch), F32)
    flat[...] = value.reshape(cols * depth, ch).astype(BF)
    wide[...] = jnp.concatenate([edge, value, edge], 0).reshape((cols + 2) * depth, ch).astype(BF)


def gather(flat, wide, r, t, tile, depth):
    parts = []
    for dc in range(3):
        for q in (r, r + 1):
            ref, at = (flat, t) if dc == 1 else (wide, t + dc * depth)
            parts.append(ref[q, pl.ds(at, tile)])
    return parts


def prepare_kernel(tile, vol, raw1, raw2, taps1, taps2, partial, again, flat, wide):
    again[...] = vol[...]
    cols, depth, ch = vol.shape[1:]
    m = cols * depth
    blank = jnp.zeros((ch, ch), BF)
    for raw, taps in ((raw1, taps1), (raw2, taps2)):
        for dc in range(3):
            quads = ((raw[0, dc], blank, raw[1, dc], raw[0, dc]), (raw[2, dc], raw[1, dc], blank, raw[2, dc]))
            for side in range(2):
                at = (side * 3 + dc) * 2 * ch
                for i in range(4):
                    taps[at + i // 2 * ch : at + (i // 2 + 1) * ch, i % 2 * ch : (i % 2 + 1) * ch] = quads[side][i]
    for r in range(2):
        spread(vol[r].astype(F32), flat.at[r], wide.at[r])
    k = 6 * ch
    for t in range(0, m, tile):
        lhs = jnp.concatenate(gather(flat, wide, 0, t, tile, depth), -1)
        for p in range(2):
            rhs = taps1[(1 - p) * k : (2 - p) * k]
            partial[p, pl.ds(t, tile)] = jnp.dot(lhs, rhs, preferred_element_type=F32)


def prepare(volume, first, second, tile=256):
    _, cols, depth, ch = volume.shape
    m = cols * depth
    return pl.pallas_call(
        functools.partial(prepare_kernel, tile),
        out_shape=[
            jax.ShapeDtypeStruct((12 * ch, 2 * ch), BF),
            jax.ShapeDtypeStruct((12 * ch, 2 * ch), BF),
            jax.ShapeDtypeStruct((2, m, 2 * ch), F32),
            jax.ShapeDtypeStruct(volume.shape, BF),
        ],
        in_specs=[vmem()] * 3,
        out_specs=[vmem()] * 4,
        scratch_shapes=[pltpu.VMEM((2, m, ch), BF), pltpu.VMEM((2, m + 2 * depth, ch), BF)],
        cost_estimate=cost(2 * 12 * ch * 2 * ch * m, 4 << 20),
        compiler_params=params(),
        name="prepare",
    )(volume, first, second)


def conv_kernel(tile, near, mid, far_a, far_b, taps1, taps2, partial, out_ref, xa, xs, ha, hs):
    cols, depth, ch = mid.shape[1:]
    m = cols * depth
    k = 6 * ch
    place = lax.axis_index("xy")
    odd = place % 2
    edge = [jnp.where(place == end, 0.0, 1.0).astype(F32) for end in (0, lax.axis_size("xy") - 1)]
    for r in range(2):
        at = 2 * (1 - odd) + r
        spread(near[r].astype(F32), xa.at[at], xs.at[at])
        at = 2 * odd + r
        spread(far_a[r].astype(F32) + far_b[r].astype(F32), xa.at[at], xs.at[at])
    blank = jnp.zeros((depth, ch), BF)
    for r in range(4):
        hs[r, pl.ds(0, depth)] = blank
        hs[r, pl.ds(m + depth, depth)] = blank
    for p in range(2):
        for t in range(0, m, tile):
            lhs = jnp.concatenate(gather(xa, xs, 2 * p, t, tile, depth), -1)
            acc = partial[p, pl.ds(t, tile)] + jnp.dot(lhs, taps1[p * k : (p + 1) * k], preferred_element_type=F32)
            h = acc * (1.0 / (1.0 + jnp.exp(-acc)))
            for half in range(2):
                r = 2 * p + half
                v = h[:, half * ch : (half + 1) * ch]
                if r in (0, 3):
                    v = v * edge[p]
                v = v.astype(BF)
                ha[r, pl.ds(t, tile)] = v
                hs[r, pl.ds(t + depth, tile)] = v
    per = cols // out_ref.shape[0]
    n = tile // depth
    for t in range(0, m, tile):
        lhs = gather(ha, hs, 0, t, tile, depth) + gather(ha, hs, 2, t, tile, depth)
        acc = jnp.dot(jnp.concatenate(lhs, -1), taps2[...], preferred_element_type=F32)
        for r in range(2):
            res = mid[r, pl.ds(t // depth, n)].astype(F32) + acc[:, r * ch : (r + 1) * ch].reshape(n, depth, ch)
            res = res.astype(BF)
            for j in range(n // per):
                out_ref[t // depth // per + j, r] = res[j * per : (j + 1) * per]


def conv_block(groups, prepared, near, mid, fars, tile=256):
    rows, cols, depth, ch = mid.shape
    m = cols * depth
    return pl.pallas_call(
        functools.partial(conv_kernel, tile),
        out_shape=jax.ShapeDtypeStruct((groups, rows, cols // groups, depth, ch), BF),
        in_specs=[vmem()] * 7,
        out_specs=vmem(),
        scratch_shapes=[
            pltpu.VMEM((4, m, ch), BF),
            pltpu.VMEM((4, m + 2 * depth, ch), BF),
            pltpu.VMEM((4, m, ch), BF),
            pltpu.VMEM((4, m + 2 * depth, ch), BF),
        ],
        cost_estimate=cost(4 * m * 12 * ch * 2 * ch, 4 << 20),
        compiler_params=params(),
        name="conv_block",
    )(near, mid, *fars, *prepared)


def attend_kernel(x_ref, wq_ref, wo_ref, out_ref):
    parts, rows, cols, depth, ch = x_ref.shape
    sect = parts * depth
    hd = ch // HEADS
    scale = 1.4426950408889634 / (hd**0.5)
    lane = lax.broadcasted_iota(jnp.int32, (1, ch), 1) // hd
    masks = [(lane == h).astype(BF) for h in range(HEADS)]
    ones = jnp.concatenate([jnp.broadcast_to(mask, (sect, ch)) for mask in masks], 0)

    def normed(r, c):
        x = x_ref[:, r, c].astype(F32).reshape(sect, ch)
        return (x * lax.rsqrt(jnp.mean(x * x, -1, keepdims=True) + 1e-6)).astype(BF)

    def scores(qkv):
        keys = jnp.concatenate([qkv[:, ch : 2 * ch] * mask for mask in masks], 0)
        return lax.dot_general(qkv[:, :ch], keys, (((1,), (1,)), ((), ())), preferred_element_type=F32)

    def weights(s):
        out = []
        for h in range(HEADS):
            part = s[:, h * sect : (h + 1) * sect]
            out.append(jnp.exp2((part - jnp.max(part, -1, keepdims=True)) * scale).astype(BF))
        return jnp.concatenate(out, 1)

    def mix(qkv, p):
        values = jnp.concatenate([qkv[:, 2 * ch :] * mask for mask in masks], 0)
        return jnp.dot(p, jnp.concatenate([values, ones], 1), preferred_element_type=F32)

    cells = [(r, c) for r in range(rows) for c in range(cols)]
    for g in range(0, len(cells), GROUP):
        some = cells[g : g + GROUP]
        n = jnp.concatenate([normed(r, c) for r, c in some], 0)
        joint = jnp.dot(n, wq_ref[...], preferred_element_type=F32).astype(BF)
        qkvs = [joint[i * sect : (i + 1) * sect] for i in range(len(some))]
        ps = [weights(s) for s in [scores(qkv) for qkv in qkvs]]
        pvs = [mix(qkv, p) for qkv, p in zip(qkvs, ps)]
        ctx = jnp.concatenate([(pv[:, :ch] / pv[:, ch:]).astype(BF) for pv in pvs], 0)
        o = jnp.dot(ctx, wo_ref[...], preferred_element_type=F32)
        for i, (r, c) in enumerate(some):
            out_ref[:, r, c] = o[i * sect : (i + 1) * sect].reshape(parts, depth, ch).astype(BF)


def attend_block(x, w_qkv, w_out):
    cells = x.shape[1] * x.shape[2]
    return pl.pallas_call(
        attend_kernel,
        out_shape=jax.ShapeDtypeStruct(x.shape, BF),
        in_specs=[vmem()] * 3,
        out_specs=vmem(),
        cost_estimate=cost(cells * 128 * 256 * 256 * 2 * 7, 1 << 20),
        compiler_params=params(),
        name="attend_block",
    )(x, w_qkv, w_out)


def finish_kernel(mixed, returned, out_ref):
    _, _, per, depth, ch = mixed.shape
    r, half = pl.program_id(0), pl.program_id(1)
    block = out_ref.shape[1]
    n = block // per
    total = mixed[pl.ds(half * n, n), r].astype(F32) + returned[pl.ds(half * n, n), r].astype(F32)
    out_ref[0] = total.astype(BF).reshape(block, depth, ch)


def finish(mixed, returned, shape, splits=2):
    rows, cols, depth, ch = shape
    return pl.pallas_call(
        finish_kernel,
        out_shape=jax.ShapeDtypeStruct(shape, BF),
        grid=(rows, splits),
        in_specs=[vmem()] * 2,
        out_specs=pl.BlockSpec((1, cols // splits, depth, ch), lambda r, s: (r, s, 0, 0)),
        cost_estimate=cost(10**6, 2 << 20),
        compiler_params=params(),
        name="finish",
    )(mixed, returned)


def swap_rows(block, pairs):
    return lax.ppermute(block, "xy", pairs)


def block(volume, conv_first, conv_second, w_qkv, w_out):
    count, groups = lax.axis_size("xy"), lax.axis_size("gz")
    links = [(i, i + 1) for i in range(1, count - 1, 2)]
    first = [pair for i, j in links[1::2] for pair in ((i, j), (j, i))]
    second = [pair for i, j in links[0::2] for pair in ((i, j), (j, i))]
    far = swap_rows(volume, first)
    near = swap_rows(volume, [(i, i ^ 1) for i in range(count)])
    *prepared, again = prepare(volume, conv_first, conv_second)
    fars = (far, swap_rows(again, second))
    mixed = conv_block(groups, prepared, near, volume, fars)
    arrived = lax.all_to_all(mixed, "gz", 0, 0, tiled=True)
    attended = attend_block(arrived, w_qkv, w_out)
    returned = lax.all_to_all(attended, "gz", 0, 0, tiled=True)
    return finish(mixed, returned, volume.shape)


def solution(mesh):
    placed = (P("xy", None, "gz", None), P(), P(), P(), P())
    return jax.shard_map(block, mesh=mesh, in_specs=placed, out_specs=P("xy", None, "gz", None), check_vma=False)
```

```python
import functools

import jax
import jax.numpy as jnp
from jax import lax
from jax.experimental import pallas as pl
from jax.experimental.pallas import tpu as pltpu
from jax.sharding import PartitionSpec as P

HEADS = 4
GROUP = 16
F32 = jnp.float32
BF = jnp.bfloat16


def vmem():
    return pl.BlockSpec(memory_space=pltpu.VMEM)


def cost(flops, moved):
    return pl.CostEstimate(flops=flops, bytes_accessed=moved, transcendentals=0)


def params():
    return pltpu.CompilerParams(vmem_limit_bytes=24 << 20)


def spread(value, flat, wide):
    cols, depth, ch = value.shape
    edge = jnp.zeros((1, depth, ch), F32)
    flat[...] = value.reshape(cols * depth, ch).astype(BF)
    wide[...] = jnp.concatenate([edge, value, edge], 0).reshape((cols + 2) * depth, ch).astype(BF)


def gather(flat, wide, r, t, tile, depth):
    parts = []
    for dc in range(3):
        for q in (r, r + 1):
            ref, at = (flat, t) if dc == 1 else (wide, t + dc * depth)
            parts.append(ref[q, pl.ds(at, tile)])
    return parts


def pack_kernel(raw1, raw2, taps1, taps2):
    ch = raw1.shape[-1]
    blank = jnp.zeros((ch, ch), BF)
    for raw, taps in ((raw1, taps1), (raw2, taps2)):
        for dc in range(3):
            quads = ((raw[0, dc], blank, raw[1, dc], raw[0, dc]), (raw[2, dc], raw[1, dc], blank, raw[2, dc]))
            for side in range(2):
                at = (side * 3 + dc) * 2 * ch
                for i in range(4):
                    taps[at + i // 2 * ch : at + (i // 2 + 1) * ch, i % 2 * ch : (i % 2 + 1) * ch] = quads[side][i]


def pack(first, second):
    ch = first.shape[-1]
    return pl.pallas_call(
        pack_kernel,
        out_shape=[jax.ShapeDtypeStruct((12 * ch, 2 * ch), BF)] * 2,
        in_specs=[vmem()] * 2,
        out_specs=[vmem()] * 2,
        cost_estimate=cost(0, 2 << 20),
        compiler_params=params(),
        name="pack",
    )(first, second)


def prepare_kernel(tile, vol, taps1, partial, mid, flat, wide):
    cols, depth, ch = vol.shape[1:]
    m = cols * depth
    k = 6 * ch
    mid[...] = vol[...]
    for r in range(2):
        spread(vol[r].astype(F32), flat.at[r], wide.at[r])
    for t in range(0, m, tile):
        lhs = jnp.concatenate(gather(flat, wide, 0, t, tile, depth), -1)
        for p in range(2):
            rhs = taps1[(1 - p) * k : (2 - p) * k]
            partial[p, pl.ds(t, tile)] = jnp.dot(lhs, rhs, preferred_element_type=F32)


def prepare(volume, taps1, tile=256):
    _, cols, depth, ch = volume.shape
    m = cols * depth
    return pl.pallas_call(
        functools.partial(prepare_kernel, tile),
        out_shape=[jax.ShapeDtypeStruct((2, m, 2 * ch), F32), jax.ShapeDtypeStruct(volume.shape, BF)],
        in_specs=[vmem()] * 2,
        out_specs=[vmem()] * 2,
        scratch_shapes=[pltpu.VMEM((2, m, ch), BF), pltpu.VMEM((2, m + 2 * depth, ch), BF)],
        cost_estimate=cost(2 * 12 * ch * 2 * ch * m, 4 << 20),
        compiler_params=params(),
        name="prepare",
    )(volume, taps1)


def hidden_side(tile, side, rows, keep, taps1, taps2, partial, xa, xs, ha, hs, emit):
    depth = (xs.shape[1] - xa.shape[1]) // 2
    m, ch = xa.shape[1:]
    k = 6 * ch
    at = pl.multiple_of(side * k, k)
    for r in range(2):
        spread(rows(r), xa.at[r], xs.at[r])
    blank = jnp.zeros((depth, ch), BF)
    for r in range(2):
        hs[r, pl.ds(0, depth)] = blank
        hs[r, pl.ds(m + depth, depth)] = blank
    for t in range(0, m, tile):
        lhs = jnp.concatenate(gather(xa, xs, 0, t, tile, depth), -1)
        acc = partial[side, pl.ds(t, tile)] + jnp.dot(lhs, taps1[pl.ds(at, k)], preferred_element_type=F32)
        h = acc * (1.0 / (1.0 + jnp.exp(-acc)))
        for r in range(2):
            v = h[:, r * ch : (r + 1) * ch]
            if keep is not None:
                v = v * jnp.where(side == r, keep, 1.0)
            v = v.astype(BF)
            ha[r, pl.ds(t, tile)] = v
            hs[r, pl.ds(t + depth, tile)] = v
    for t in range(0, m, tile):
        lhs = jnp.concatenate(gather(ha, hs, 0, t, tile, depth), -1)
        emit(t, jnp.dot(lhs, taps2[pl.ds(at, k)], preferred_element_type=F32))


def side_scratch(m, depth, ch):
    return [pltpu.VMEM((2, n, ch), BF) for n in (m, m + 2 * depth) * 2]


def near_kernel(tile, near, taps1, taps2, partial, half, *scratch):
    def emit(t, acc):
        half[pl.ds(t, tile)] = acc

    side = 1 - lax.axis_index("xy") % 2
    hidden_side(tile, side, lambda r: near[r].astype(F32), None, taps1, taps2, partial, *scratch, emit)


def near_block(near, taps1, taps2, partial, tile=256):
    _, cols, depth, ch = near.shape
    m = cols * depth
    return pl.pallas_call(
        functools.partial(near_kernel, tile),
        out_shape=jax.ShapeDtypeStruct((m, 2 * ch), F32),
        in_specs=[vmem()] * 4,
        out_specs=vmem(),
        scratch_shapes=side_scratch(m, depth, ch),
        cost_estimate=cost(2 * m * 12 * ch * 2 * ch, 2 << 20),
        compiler_params=params(),
        name="near_block",
    )(near, taps1, taps2, partial)


def far_kernel(tile, far_a, far_b, mid, taps1, taps2, partial, half, out_ref, *scratch):
    cols, depth, ch = mid.shape[1:]
    per = cols // out_ref.shape[0]
    n = tile // depth
    place = lax.axis_index("xy")
    inside = (place > 0) & (place < lax.axis_size("xy") - 1)

    def rows(r):
        return far_a[r].astype(F32) + far_b[r].astype(F32)

    def emit(t, acc):
        acc = acc + half[pl.ds(t, tile)]
        for r in range(2):
            res = mid[r, pl.ds(t // depth, n)].astype(F32) + acc[:, r * ch : (r + 1) * ch].reshape(n, depth, ch)
            res = res.astype(BF)
            for j in range(n // per):
                out_ref[t // depth // per + j, r] = res[j * per : (j + 1) * per]

    keep = jnp.where(inside, 1.0, 0.0).astype(F32)
    hidden_side(tile, place % 2, rows, keep, taps1, taps2, partial, *scratch, emit)


def far_block(groups, fars, mid, taps1, taps2, partial, half, tile=256):
    rows, cols, depth, ch = mid.shape
    m = cols * depth
    return pl.pallas_call(
        functools.partial(far_kernel, tile),
        out_shape=jax.ShapeDtypeStruct((groups, rows, cols // groups, depth, ch), BF),
        in_specs=[vmem()] * 7,
        out_specs=vmem(),
        scratch_shapes=side_scratch(m, depth, ch),
        cost_estimate=cost(2 * m * 12 * ch * 2 * ch, 2 << 20),
        compiler_params=params(),
        name="far_block",
    )(*fars, mid, taps1, taps2, partial, half)


def attend_kernel(x_ref, wq_ref, wo_ref, out_ref):
    parts, rows, cols, depth, ch = x_ref.shape
    sect = parts * depth
    hd = ch // HEADS
    scale = 1.4426950408889634 / (hd**0.5)
    lane = lax.broadcasted_iota(jnp.int32, (1, ch), 1) // hd
    masks = [(lane == h).astype(BF) for h in range(HEADS)]
    ones = jnp.concatenate([jnp.broadcast_to(mask, (sect, ch)) for mask in masks], 0)

    def normed(r, c):
        x = x_ref[:, r, c].astype(F32).reshape(sect, ch)
        return (x * lax.rsqrt(jnp.mean(x * x, -1, keepdims=True) + 1e-6)).astype(BF)

    def scores(qkv):
        keys = jnp.concatenate([qkv[:, ch : 2 * ch] * mask for mask in masks], 0)
        return lax.dot_general(qkv[:, :ch], keys, (((1,), (1,)), ((), ())), preferred_element_type=F32)

    def weights(s):
        out = []
        for h in range(HEADS):
            part = s[:, h * sect : (h + 1) * sect]
            out.append(jnp.exp2((part - jnp.max(part, -1, keepdims=True)) * scale).astype(BF))
        return jnp.concatenate(out, 1)

    def mix(qkv, p):
        values = jnp.concatenate([qkv[:, 2 * ch :] * mask for mask in masks], 0)
        return jnp.dot(p, jnp.concatenate([values, ones], 1), preferred_element_type=F32)

    cells = [(r, c) for r in range(rows) for c in range(cols)]
    for g in range(0, len(cells), GROUP):
        some = cells[g : g + GROUP]
        n = jnp.concatenate([normed(r, c) for r, c in some], 0)
        joint = jnp.dot(n, wq_ref[...], preferred_element_type=F32).astype(BF)
        qkvs = [joint[i * sect : (i + 1) * sect] for i in range(len(some))]
        ps = [weights(s) for s in [scores(qkv) for qkv in qkvs]]
        pvs = [mix(qkv, p) for qkv, p in zip(qkvs, ps)]
        ctx = jnp.concatenate([(pv[:, :ch] / pv[:, ch:]).astype(BF) for pv in pvs], 0)
        o = jnp.dot(ctx, wo_ref[...], preferred_element_type=F32)
        for i, (r, c) in enumerate(some):
            part = o[i * sect : (i + 1) * sect].reshape(parts, depth, ch).astype(BF)
            out_ref[:, r, c] = (x_ref[:, r, c].astype(F32) + part.astype(F32)).astype(BF)


def attend_block(x, w_qkv, w_out):
    cells = x.shape[1] * x.shape[2]
    return pl.pallas_call(
        attend_kernel,
        out_shape=jax.ShapeDtypeStruct(x.shape, BF),
        in_specs=[vmem()] * 3,
        out_specs=vmem(),
        cost_estimate=cost(cells * 128 * 256 * 256 * 2 * 7, 1 << 20),
        compiler_params=params(),
        name="attend_block",
    )(x, w_qkv, w_out)


def finish_kernel(splits, source, target, sems):
    groups = source.shape[0]
    n = groups // splits
    copies = [
        pltpu.make_async_copy(
            source.at[pl.ds(s * n, n), r], target.at[r, pl.ds(s * n, n)], sems.at[r * splits + s]
        )
        for r in range(source.shape[1])
        for s in range(splits)
    ]
    for copy in copies:
        copy.start()
    for copy in copies:
        copy.wait()


def finish(refined, shape, splits=1):
    groups, rows, per, depth, ch = refined.shape
    return pl.pallas_call(
        functools.partial(finish_kernel, splits),
        out_shape=jax.ShapeDtypeStruct((rows, groups, per, depth, ch), BF),
        in_specs=[vmem()],
        out_specs=pl.BlockSpec(memory_space=pltpu.HBM),
        scratch_shapes=[pltpu.SemaphoreType.DMA((rows * splits,))],
        cost_estimate=cost(0, 1 << 20),
        compiler_params=params(),
        name="finish",
    )(refined).reshape(shape)


def swap_rows(block, pairs):
    return lax.ppermute(block, "xy", pairs)


def exchange(parts, groups):
    far = groups // 4
    order = [2 * (y + hop) + half for half in range(2) for y in range(far) for hop in (0, far)]
    return lax.all_to_all(parts, "gz", 0, 0, tiled=True, axis_index_groups=[order])


def block(volume, conv_first, conv_second, w_qkv, w_out):
    count, groups = lax.axis_size("xy"), lax.axis_size("gz")
    far_odd = swap_rows(volume, [(i, i - 1) for i in range(2, count, 2)])
    near = swap_rows(volume, [(i, i ^ 1) for i in range(count)])
    taps1, taps2 = pack(conv_first, conv_second)
    far_even = swap_rows(near, [(i, i + 2) for i in range(0, count - 2, 2)])
    fars = (far_odd, far_even)
    partial, mid = prepare(volume, taps1)
    half = near_block(near, taps1, taps2, partial)
    mixed = far_block(groups, fars, mid, taps1, taps2, partial, half)
    arrived = exchange(mixed, groups)
    attended = attend_block(arrived, w_qkv, w_out)
    returned = exchange(attended, groups)
    return finish(returned, volume.shape)


def solution(mesh):
    placed = (P("xy", None, "gz", None), P(), P(), P(), P())
    return jax.shard_map(block, mesh=mesh, in_specs=placed, out_specs=P("xy", None, "gz", None), check_vma=False)
```
